32 devices in a mesh: task: 16 (over z, y, x), shard: 2 (over core).
Axes of the slice: x: 2, y: 2, z: 4, core: 2. Of those that a mesh axis runs over, the one named last changes fastest.
Arguments:
- tokens: bfloat16 [16, 512, 1024], P('task'), may hold values from -6 to 6
- targets: bfloat16 [16, 512, 1024], P('task'), may hold values from -6 to 6
- meta_tokens: bfloat16 [16, 512, 1024], P('task'), may hold values from -6 to 6
- meta_targets: bfloat16 [16, 512, 1024], P('task'), may hold values from -6 to 6
- gate_weight: bfloat16 [16, 1024, 1536], P('task', None, 'shard'), may hold values from -0.1875 to 0.1875
- up_weight: bfloat16 [16, 1024, 1536], P('task', None, 'shard'), may hold values from -0.1875 to 0.1875
- down_weight: bfloat16 [16, 1536, 1024], P('task', 'shard'), may hold values from -0.15625 to 0.15625
- task_step: int32 [16], P('task'), may hold values from 0 to 9999
- hidden_state: float32 [16, 3, 512], P('task'), may hold values from -3 to 3
- cell_state: float32 [16, 3, 512], P('task'), may hold values from -6 to 6
- recurrent_weight: float32 [512, 2048], P('task'), may hold values from -0.25 to 0.25
- input_weight: float32 [3, 2048], replicated, may hold values from -3.5 to 3.5
- lstm_bias: float32 [2048], replicated, may hold values from -3 to 3
- context_weight: float32 [512, 5], replicated, may hold values from -0.25 to 0.25
- mlp_weight: float32 [3, 4], replicated, may hold values from -4 to 4
Outputs:
- gate_update: bfloat16 [16, 1024, 1536], P('task', None, 'shard')
- up_update: bfloat16 [16, 1024, 1536], P('task', None, 'shard')
- down_update: bfloat16 [16, 1536, 1024], P('task', 'shard')
- new_hidden: float32 [16, 3, 512], P('task')
- new_cell: float32 [16, 3, 512], P('task')
- meta_loss: float32 [], replicated
The draws below stay inside these ranges and needn't reach their ends.
All inputs are finite; a program needn't handle non-finite values.
Results may differ from the reference program's by a relative error of at most 0.0056.
Values sent between devices are 32-bit elements; how exact they have to be, the bound alone decides.
A program may use at most 128 MiB of HBM per device.

```python
import jax
import jax.numpy as jnp
from jax import lax

D = 1024
FF = 1536
H = 512
MLP_H = 4
FEAT = 3
STEPS = 10000
TOK = 512
TASKS = 16


def touch_ends(array, own_key, smallest, top_value):
    dims = array.shape
    spot = [jax.random.randint(jax.random.fold_in(own_key, axis), (), 0, dims[axis]) for axis in range(len(dims))]
    array = array.at[tuple(spot)].set(smallest)
    longest = dims.index(max(dims))
    spot[longest] = (spot[longest] + 1) % dims[longest]
    return array.at[tuple(spot)].set(top_value)


def block_scale(rng, extent, shards, low, top_value):
    factor_of, own = 1.0, jax.random.fold_in(rng, 6)
    for dim, shards_of in shards:
        steps = jnp.exp(jax.random.uniform(jax.random.fold_in(own, dim), (shards_of,), jnp.float32, low / len(shards), top_value / len(shards)))
        factor_of = factor_of * jnp.repeat(steps, extent[dim] // shards_of).reshape([-1 if axis == dim else 1 for axis in range(len(extent))])
    return factor_of


def gaussian(own_key, dims, scale, reach, split=(), kind=jnp.bfloat16):
    drawn = jax.random.normal(own_key, dims, jnp.float32) * scale
    if len(split) > 0:
        drawn = block_scale(own_key, dims, split, -0.22, 0.18) * drawn
    return jnp.clip(drawn, min=-reach, max=reach).astype(kind)


def setup_inputs(seed: int = 0) -> dict:
    key_of = jax.random.split(jax.random.key(seed), 16)
    tokens = gaussian(key_of[0], (TASKS, TOK, D), 1.0, 6.0, ((0, 16),))
    targets = gaussian(key_of[1], (TASKS, TOK, D), 1.0, 6.0, ((0, 16),))
    meta_tokens = gaussian(key_of[2], (TASKS, TOK, D), 1.0, 6.0, ((0, 16),))
    meta_targets = gaussian(key_of[3], (TASKS, TOK, D), 1.0, 6.0, ((0, 16),))
    gate_weight = gaussian(key_of[4], (TASKS, D, FF), D ** -0.5, 0.1875, ((0, 16), (2, 2)))
    up_weight = gaussian(key_of[5], (TASKS, D, FF), D ** -0.5, 0.1875, ((0, 16), (2, 2)))
    down_weight = gaussian(key_of[6], (TASKS, FF, D), FF ** -0.5, 0.15625, ((0, 16), (1, 2)))
    task_step = touch_ends(jax.random.randint(key_of[7], (TASKS,), 0, STEPS), jax.random.fold_in(key_of[7], 1), 0, STEPS - 1).astype(jnp.int32)
    hidden_state = gaussian(key_of[8], (TASKS, 3, H), 0.5, 3.0, ((0, 16),), jnp.float32)
    cell_state = gaussian(key_of[9], (TASKS, 3, H), 1.0, 6.0, ((0, 16),), jnp.float32)
    recurrent_weight = gaussian(key_of[10], (H, 4 * H), H ** -0.5, 0.25, ((0, 16),), jnp.float32)
    input_weight = gaussian(key_of[11], (FEAT, 4 * H), FEAT ** -0.5, 3.5, (), jnp.float32)
    lstm_bias = gaussian(key_of[12], (4 * H,), 0.5, 3.0, (), jnp.float32)
    context_weight = gaussian(key_of[13], (H, MLP_H + 1), H ** -0.5, 0.25, (), jnp.float32)
    mlp_weight = gaussian(key_of[14], (3, MLP_H), 1.0, 4.0, (), jnp.float32)
    return dict(tokens=tokens, targets=targets, meta_tokens=meta_tokens, meta_targets=meta_targets, gate_weight=gate_weight, up_weight=up_weight, down_weight=down_weight, task_step=task_step, hidden_state=hidden_state, cell_state=cell_state, recurrent_weight=recurrent_weight, input_weight=input_weight, lstm_bias=lstm_bias, context_weight=context_weight, mlp_weight=mlp_weight)


highest = lax.Precision.HIGHEST
epsilon = 1e-06
rate_factor = 0.1

def block_forward(inputs, w_gate, w_up, w_down):
    gate_pre = jnp.dot(inputs, w_gate, preferred_element_type=jnp.float32)
    up_pre = jnp.dot(inputs, w_up, preferred_element_type=jnp.float32)
    sigmoid_gate = jax.nn.sigmoid(gate_pre)
    activated = (gate_pre * sigmoid_gate * up_pre).astype(jnp.bfloat16)
    output = jnp.dot(activated, w_down, preferred_element_type=jnp.float32)
    return (gate_pre, up_pre, sigmoid_gate, activated, output)

def block_grads(inputs, w_down, gate_pre, up_pre, sigmoid_gate, activated, d_out):
    d_act = lax.dot_general(d_out, w_down, (((1,), (1,)), ((), ())), preferred_element_type=jnp.float32)
    d_gate = (d_act * up_pre * sigmoid_gate * (1.0 + gate_pre * (1.0 - sigmoid_gate))).astype(jnp.bfloat16)
    d_up = (d_act * gate_pre * sigmoid_gate).astype(jnp.bfloat16)
    grad_gate = lax.dot_general(inputs, d_gate, (((0,), (0,)), ((), ())), preferred_element_type=jnp.float32)
    grad_up = lax.dot_general(inputs, d_up, (((0,), (0,)), ((), ())), preferred_element_type=jnp.float32)
    grad_down = lax.dot_general(activated, d_out, (((0,), (0,)), ((), ())), preferred_element_type=jnp.float32)
    return (grad_gate, grad_up, grad_down)

def lstm_step(features, recurrent_term, cell_old, input_weight, lstm_bias, context_weight):
    state_width = cell_old.shape[-1]
    lstm_in = jnp.dot(features, input_weight, precision=highest) + recurrent_term + lstm_bias
    in_gate = jax.nn.sigmoid(lstm_in[:, :state_width])
    forget_gate = jax.nn.sigmoid(lstm_in[:, state_width:2 * state_width])
    candidate = jnp.tanh(lstm_in[:, 2 * state_width:3 * state_width])
    out_gate = jax.nn.sigmoid(lstm_in[:, 3 * state_width:])
    cell_new = forget_gate * cell_old + in_gate * candidate
    hidden_new = out_gate * jnp.tanh(cell_new)
    context = jnp.dot(hidden_new, context_weight, precision=highest)
    return (hidden_new, cell_new, context)

def param_update(param, gradient, rms_param, rms_grad, context_row, mlp_weight):
    p_norm = param.astype(jnp.float32) / rms_param
    g_norm = gradient / rms_grad
    summed = jnp.zeros(param.shape, jnp.float32)
    for hidden_unit in range(mlp_weight.shape[1]):
        inner = mlp_weight[0, hidden_unit] * p_norm + mlp_weight[1, hidden_unit] * g_norm + context_row[hidden_unit]
        summed = summed + mlp_weight[2, hidden_unit] * jax.nn.relu(inner)
    update = jnp.exp(context_row[-1]) * summed
    new_param = (param.astype(jnp.float32) - rate_factor * rms_param * update).astype(jnp.bfloat16)
    return (update.astype(jnp.bfloat16), new_param)

def reference(tokens, targets, meta_tokens, meta_targets, gate_weight, up_weight, down_weight, task_step, hidden_state, cell_state, recurrent_weight, input_weight, lstm_bias, context_weight, mlp_weight):

    def one_task(operands):
        inputs, wanted, meta_in, meta_want, w_gate, w_up, w_down, step_now, hidden_old, cell_old = operands
        gate_pre, up_pre, sigmoid_gate, activated, output = block_forward(inputs, w_gate, w_up, w_down)
        d_out = (output - wanted.astype(jnp.float32)).astype(jnp.bfloat16)
        gradients = block_grads(inputs, w_down, gate_pre, up_pre, sigmoid_gate, activated, d_out)
        params = (w_gate, w_up, w_down)
        entries = float(D * FF)
        grad_sq = jnp.stack([jnp.sum(grad_piece * grad_piece) for grad_piece in gradients])
        param_sq = jnp.stack([jnp.sum(jnp.square(param_piece.astype(jnp.float32))) for param_piece in params])
        rms_grad = jnp.sqrt(grad_sq / entries + epsilon)
        rms_param = jnp.sqrt(param_sq / entries + epsilon)
        fraction = jnp.full((3,), step_now.astype(jnp.float32) / STEPS, jnp.float32)
        features = jnp.stack([jnp.log(rms_grad), jnp.log(rms_param), fraction], axis=1)
        recurrent_term = jnp.dot(hidden_old, recurrent_weight, precision=highest)
        hidden_new, cell_new, context = lstm_step(features, recurrent_term, cell_old, input_weight, lstm_bias, context_weight)
        results = [param_update(params[tensor_id], gradients[tensor_id], rms_param[tensor_id], rms_grad[tensor_id], context[tensor_id], mlp_weight) for tensor_id in range(3)]
        meta_out = block_forward(meta_in, results[0][1], results[1][1], results[2][1])[4]
        meta_part = 0.5 * jnp.sum(jnp.square(meta_out - meta_want.astype(jnp.float32))) / (TOK * D)
        return (results[0][0], results[1][0], results[2][0], hidden_new, cell_new, meta_part)
    gate_update, up_update, down_update, new_hidden, new_cell, meta_parts = lax.map(one_task, (tokens, targets, meta_tokens, meta_targets, gate_weight, up_weight, down_weight, task_step, hidden_state, cell_state))
    meta_loss = jnp.sum(meta_parts) / TASKS
    return (gate_update, up_update, down_update, new_hidden, new_cell, meta_loss)
```

```python
import functools

import jax
import jax.numpy as jnp
from jax import lax
from jax.experimental import pallas as pl
from jax.experimental.pallas import tpu as pltpu
from jax.sharding import PartitionSpec as P

STEPS = 10000

highest = lax.Precision.HIGHEST
epsilon = 1e-06
rate_factor = 0.1
f32 = jnp.float32
bf16 = jnp.bfloat16
MESH = pl.DeviceIdType.MESH


def dot(a, b, dims=((1,), (0,)), precision=None):
    return lax.dot_general(a, b, (dims, ((), ())), preferred_element_type=f32, precision=precision)


def fold_sq(x):
    x = x * x
    return jnp.sum(x.reshape(x.shape[0] // 8, 8, x.shape[1]), axis=0)


def total(x):
    return jnp.sum(jnp.sum(x, axis=1, keepdims=True), axis=0, keepdims=True)


def kernel(
    n,
    tok_hbm, tgt_hbm, mtok_hbm, mtgt_hbm, gate_hbm, up_hbm, down_hbm,
    step_ref, hid_ref, cell_ref, rw_ref, iw_ref, bias_ref, cw_ref, mlp_ref,
    gu_hbm, uu_hbm, du_hbm, nh_ref, nc_ref, loss_ref,
    tok, tgt, mtok, mtgt, gate, up, down,
    fa, fb, act, part, recv, tok_t, act_t, dout, dgate, dup,
    gg, gu, gd, ug, uu, ud, msend, mown, mrecv,
    hid_pad, hid_all, rec_part, rec_recv, rec_half, rec_full, sq, stat, stat_recv, cell_pad,
    lossv, loss_recv, loss_chip, loss_all,
    in_sem, out_sem, hid_s, hid_r, rec_s, rec_r, loss_s, loss_r, sib_s, sib_r,
):
    me = lax.axis_index("task")
    core = lax.axis_index("shard")
    sib = 1 - core
    toks, width = tok.shape
    ff = gate.shape[1]
    h = hid_pad.shape[1]
    r = rw_ref.shape[0]
    tb = toks // 2
    fbk = 256
    half = rec_half.shape[1]

    barrier = pltpu.get_barrier_semaphore()

    def peer(off):
        return lax.rem(me + off, n)

    @pl.loop(1, n)
    def _(off):
        pl.semaphore_signal(barrier, inc=1, device_id=(peer(off), core), device_id_type=MESH)

    pl.semaphore_signal(barrier, inc=1, device_id=(me, sib), device_id_type=MESH)

    ins = [
        pltpu.make_async_copy(src.at[0], dst, in_sem.at[i])
        for i, (src, dst) in enumerate(
            ((tok_hbm, tok), (gate_hbm, gate), (up_hbm, up), (down_hbm, down), (tgt_hbm, tgt), (mtok_hbm, mtok), (mtgt_hbm, mtgt))
        )
    ]
    for c in ins:
        c.start()

    hid_pad[...] = jnp.zeros_like(hid_pad)
    hid_pad[0:3, :] = hid_ref[0]
    cell_pad[...] = jnp.zeros_like(cell_pad)
    cell_pad[0:3, :] = cell_ref[0]
    sq[...] = jnp.zeros_like(sq)
    hid_all[me] = hid_pad[...]

    def to_task(src, dst, ss, rs, who, slot):
        return pltpu.make_async_remote_copy(
            src_ref=src, dst_ref=dst.at[slot], send_sem=ss.at[who], recv_sem=rs.at[slot],
            device_id=(who, core), device_id_type=MESH,
        )

    def to_sib(src, dst, i):
        return pltpu.make_async_remote_copy(
            src_ref=src, dst_ref=dst, send_sem=sib_s.at[i], recv_sem=sib_r.at[i],
            device_id=(me, sib), device_id_type=MESH,
        )

    pl.semaphore_wait(barrier, n)

    @pl.loop(1, n)
    def _(off):
        to_task(hid_pad, hid_all, hid_s, hid_r, peer(off), me).start()

    ins[0].wait()
    ins[1].wait()
    ins[2].wait()

    def hidden(x, w1, w2, keep):
        @pl.loop(0, ff // fbk)
        def _(j):
            fs = pl.ds(pl.multiple_of(j * fbk, fbk), fbk)
            for i in range(2):
                ts = pl.ds(i * tb, tb)
                g = dot(x[ts, :], w1[:, fs])
                u = dot(x[ts, :], w2[:, fs])
                s = jax.nn.sigmoid(g)
                a = g * s
                act[ts, fs] = (a * u).astype(bf16)
                if keep:
                    fa[ts, fs] = a
                    fb[ts, fs] = u * s * (1.0 + g * (1.0 - s))

    hidden(tok, gate, up, True)
    ins[3].wait()
    for i in range(2):
        part[i] = dot(act[pl.ds(i * tb, tb), :], down[...])
        to_sib(part.at[i], recv.at[i], i).start()

    @pl.loop(1, n)
    def _(off):
        s = peer(off)
        to_task(hid_pad, hid_all, hid_s, hid_r, s, s).wait_recv()

    picks = lax.broadcasted_iota(jnp.int32, (h, r), 0) == lax.broadcasted_iota(jnp.int32, (h, r), 1) + me * r
    mine = dot(hid_all[...].reshape(n * 8, h), picks.astype(f32), precision=highest)
    cols = pl.ds(pl.multiple_of(core * half, half), half)
    rec_part[...] = dot(mine, rw_ref[:, cols], precision=highest).reshape(n, 8, half)

    @pl.loop(1, n)
    def _(off):
        s = peer(off)
        to_task(rec_part.at[s], rec_recv, rec_s, rec_r, s, me).start()

    rec_recv[me] = rec_part[me]

    tok_t[...] = tok[...].T
    act_t[...] = act[...].T

    def param_sq(w, slot):
        @pl.loop(0, w.shape[0] // 64)
        def _(k):
            x = w[pl.ds(pl.multiple_of(k * 64, 64), 64), :].astype(f32)
            x = fold_sq(x)
            sq[slot] += sum(x[:, q * fbk:(q + 1) * fbk] for q in range(x.shape[1] // fbk))

    param_sq(gate, 3)
    param_sq(up, 4)
    param_sq(down, 5)

    ins[4].wait()
    for i in range(2):
        to_sib(part.at[i], recv.at[i], i).wait()
        ts = pl.ds(i * tb, tb)

        @pl.loop(0, tb // 16)
        def _(k):
            rows = pl.ds(pl.multiple_of(k * 16, 16), 16)
            whole = pl.ds(pl.multiple_of(i * tb + k * 16, 16), 16)
            dout[whole, :] = (part[i, rows, :] + recv[i, rows, :] - tgt[whole, :].astype(f32)).astype(bf16)

        @pl.loop(0, ff // fbk)
        def _(j):
            fs = pl.ds(pl.multiple_of(j * fbk, fbk), fbk)
            d_act = dot(dout[ts, :], down[fs, :], ((1,), (1,)))
            dgate[ts, fs] = (d_act * fb[ts, fs]).astype(bf16)
            dup[ts, fs] = (d_act * fa[ts, fs]).astype(bf16)

    def grad(lhs, rhs, out, slot):
        @pl.loop(0, rhs.shape[1] // fbk)
        def _(j):
            fs = pl.ds(pl.multiple_of(j * fbk, fbk), fbk)
            for q in range(lhs.shape[0] // 256):
                rows = pl.ds(q * 256, 256)
                g = dot(lhs[rows, :], rhs[:, fs])
                out[rows, fs] = g
                sq[slot] += fold_sq(g)

    grad(tok_t, dgate, gg, 0)
    grad(tok_t, dup, gu, 1)
    grad(act_t, dout, gd, 2)

    stat[...] = jnp.zeros_like(stat)
    for i in range(6):
        stat[i // 3, i % 3:i % 3 + 1, :] = jnp.broadcast_to(total(sq[i]), (1, 128))
    to_sib(stat, stat_recv, 2).start()

    @pl.loop(1, n)
    def _(off):
        s = peer(off)
        to_task(rec_part.at[s], rec_recv, rec_s, rec_r, s, s).wait_recv()

    rec_half[...] = jnp.sum(rec_recv[...], axis=0)
    to_sib(rec_half, rec_full.at[core], 3).start()
    rec_full[core] = rec_half[...]

    to_sib(stat, stat_recv, 2).wait()
    entries = 2.0 * (width * ff)
    rms = jnp.sqrt((stat[...] + stat_recv[...]) / entries + epsilon)
    rms_g, rms_p = rms[0], rms[1]
    lg, lp = jnp.log(rms_g)[:, 0:1], jnp.log(rms_p)[:, 0:1]
    frac = step_ref[0].astype(f32) / STEPS
    pltpu.make_async_remote_copy(
        src_ref=rec_half, dst_ref=rec_full.at[sib], send_sem=sib_s.at[3], recv_sem=sib_r.at[3],
        device_id=(me, sib), device_id_type=MESH,
    ).wait()

    def block(q):
        qs = pl.ds(q * h, h)
        rec = rec_full[(q * h) // half, :, pl.ds((q * h) % half, h)]
        return lg * iw_ref[0:1, qs] + lp * iw_ref[1:2, qs] + frac * iw_ref[2:3, qs] + rec + bias_ref[0:1, qs]

    cell = jax.nn.sigmoid(block(1)) * cell_pad[...] + jax.nn.sigmoid(block(0)) * jnp.tanh(block(2))
    hid = jax.nn.sigmoid(block(3)) * jnp.tanh(cell)
    nc_ref[0] = cell[0:3]
    nh_ref[0] = hid[0:3]
    ctx = dot(hid, cw_ref[...], precision=highest)

    units = mlp_ref.shape[1]

    def update(t, w, g, out, out_hbm):
        rp, rg = rms_p[t:t + 1, 0:1], rms_g[t:t + 1, 0:1]
        ca = [mlp_ref[0, k] / rp for k in range(units)]
        cb = [mlp_ref[1, k] / rg for k in range(units)]
        cc = [ctx[t:t + 1, k:k + 1] for k in range(units)]
        size = jnp.exp(ctx[t:t + 1, units:units + 1])
        back = rate_factor * rp

        @pl.loop(0, w.shape[0] // 16)
        def _(i):
            rows = pl.ds(pl.multiple_of(i * 16, 16), 16)
            p = w[rows, :].astype(f32)
            gv = g[rows, :]
            acc = None
            for k in range(units):
                term = mlp_ref[2, k] * jnp.maximum(ca[k] * p + cb[k] * gv + cc[k], 0.0)
                acc = term if acc is None else acc + term
            upd = size * acc
            out[rows, :] = upd.astype(bf16)
            w[rows, :] = (p - back * upd).astype(bf16)

        return pltpu.make_async_copy(out, out_hbm.at[0], out_sem.at[t])

    outs = []
    for t, (w, g, o, oh) in enumerate(((gate, gg, ug, gu_hbm), (up, gu, uu, uu_hbm), (down, gd, ud, du_hbm))):
        c = update(t, w, g, o, oh)
        c.start()
        outs.append(c)

    ins[5].wait()
    hidden(mtok, gate, up, False)
    msend[...] = dot(act[pl.ds(pl.multiple_of(sib * tb, tb), tb), :], down[...])
    to_sib(msend, mrecv, 4).start()
    own = pl.multiple_of(core * tb, tb)
    mown[...] = dot(act[pl.ds(own, tb), :], down[...])
    ins[6].wait()
    to_sib(msend, mrecv, 4).wait()
    lossv[...] = jnp.zeros_like(lossv)

    @pl.loop(0, tb // 16)
    def _(k):
        rows = pl.ds(pl.multiple_of(k * 16, 16), 16)
        d = mown[rows, :] + mrecv[rows, :] - mtgt[pl.ds(pl.multiple_of(own + k * 16, 16), 16), :].astype(f32)
        d = fold_sq(d)
        lossv[...] += sum(d[:, q * 128:(q + 1) * 128] for q in range(width // 128))

    to_sib(lossv, loss_recv, 5).start()
    to_sib(lossv, loss_recv, 5).wait()
    chip = lossv[...] + loss_recv[...]
    loss_chip[...] = chip
    loss_all[me] = chip

    @pl.loop(1, n)
    def _(off):
        to_task(loss_chip, loss_all, loss_s, loss_r, peer(off), me).start()

    for c in outs:
        c.wait()

    @pl.loop(1, n)
    def _(off):
        s = peer(off)
        to_task(hid_pad, hid_all, hid_s, hid_r, s, me).wait_send()
        to_task(rec_part.at[s], rec_recv, rec_s, rec_r, s, me).wait_send()
        to_task(loss_chip, loss_all, loss_s, loss_r, s, me).wait_send()
        to_task(loss_chip, loss_all, loss_s, loss_r, s, s).wait_recv()

    loss_ref[0, 0] = jnp.sum(jnp.sum(loss_all[...], axis=0)) * (0.5 / (toks * width)) / n


def local(*args):
    n = lax.axis_size("task")
    (tokens, targets, mtokens, mtargets, gate, up, down, step, hid, cell, rw, iw, bias, cw, mlp) = args
    toks, width = tokens.shape[1:]
    ff = gate.shape[2]
    h = hid.shape[2]
    r = rw.shape[0]
    half = rw.shape[1] // 2
    vm = pl.BlockSpec(memory_space=pltpu.VMEM)
    sm = pl.BlockSpec(memory_space=pltpu.SMEM)
    anys = pl.BlockSpec(memory_space=pl.ANY)
    V = pltpu.VMEM
    dma = pltpu.SemaphoreType.DMA
    tb = toks // 2
    outs = pl.pallas_call(
        functools.partial(kernel, n),
        out_shape=(
            jax.ShapeDtypeStruct(gate.shape, bf16),
            jax.ShapeDtypeStruct(up.shape, bf16),
            jax.ShapeDtypeStruct(down.shape, bf16),
            jax.ShapeDtypeStruct(hid.shape, f32),
            jax.ShapeDtypeStruct(cell.shape, f32),
            jax.ShapeDtypeStruct((1, 1), f32),
        ),
        in_specs=[anys] * 7 + [sm] + [vm] * 6 + [sm],
        out_specs=(anys, anys, anys, vm, vm, sm),
        scratch_shapes=[
            V((toks, width), bf16), V((toks, width), bf16), V((toks, width), bf16), V((toks, width), bf16),
            V((width, ff), bf16), V((width, ff), bf16), V((ff, width), bf16),
            V((toks, ff), f32), V((toks, ff), f32), V((toks, ff), bf16),
            V((2, tb, width), f32), V((2, tb, width), f32),
            V((width, toks), bf16), V((ff, toks), bf16), V((toks, width), bf16),
            V((toks, ff), bf16), V((toks, ff), bf16),
            V((width, ff), f32), V((width, ff), f32), V((ff, width), f32),
            V((width, ff), bf16), V((width, ff), bf16), V((ff, width), bf16),
            V((tb, width), f32), V((tb, width), f32), V((tb, width), f32),
            V((8, h), f32), V((n, 8, h), f32), V((n, 8, half), f32), V((n, 8, half), f32),
            V((8, half), f32), V((2, 8, half), f32),
            V((6, 8, 256), f32), V((2, 8, 128), f32), V((2, 8, 128), f32), V((8, h), f32),
            V((8, 128), f32), V((8, 128), f32), V((8, 128), f32), V((n, 8, 128), f32),
            dma((7,)), dma((3,)), dma((n,)), dma((n,)), dma((n,)), dma((n,)), dma((n,)), dma((n,)),
            dma((6,)), dma((6,)),
        ],
        compiler_params=pltpu.CompilerParams(
            collective_id=0, has_side_effects=True, vmem_limit_bytes=62 * 1024 * 1024
        ),
    )(tokens, targets, mtokens, mtargets, gate, up, down, step, hid, cell, rw, iw, bias[None], cw, mlp)
    return (*outs[:5], outs[5][0, 0])


def solution(mesh):
    return jax.shard_map(
        local,
        mesh=mesh,
        in_specs=(
            P("task", None, None),
            P("task", None, None),
            P("task", None, None),
            P("task", None, None),
            P("task", None, "shard"),
            P("task", None, "shard"),
            P("task", "shard", None),
            P("task"),
            P("task", None, None),
            P("task", None, None),
            P("task", None),
            P(),
            P(),
            P(),
            P(),
        ),
        out_specs=(
            P("task", None, "shard"),
            P("task", None, "shard"),
            P("task", "shard", None),
            P("task", None, None),
            P("task", None, None),
            P(),
        ),
        check_vma=False,
    )
```

```python
import functools

import jax
import jax.numpy as jnp
from jax import lax
from jax.experimental import pallas as pl
from jax.experimental.pallas import tpu as pltpu
from jax.sharding import PartitionSpec as P

STEPS = 10000

highest = lax.Precision.HIGHEST
epsilon = 1e-06
rate_factor = 0.1
f32 = jnp.float32
bf16 = jnp.bfloat16
MESH = pl.DeviceIdType.MESH


def dot(a, b, dims=((1,), (0,)), precision=None):
    return lax.dot_general(a, b, (dims, ((), ())), preferred_element_type=f32, precision=precision)


def fold_sq(x):
    x = x * x
    return jnp.sum(x.reshape(x.shape[0] // 8, 8, x.shape[1]), axis=0)


def total(x):
    return jnp.sum(jnp.sum(x, axis=1, keepdims=True), axis=0, keepdims=True)


def kernel(
    n,
    tok_hbm, tgt_hbm, mtok_hbm, mtgt_hbm, gate_hbm, up_hbm, down_hbm,
    step_ref, hid_ref, cell_ref, rw_ref, iw_ref, bias_ref, cw_ref, mlp_ref,
    gu_hbm, uu_hbm, du_hbm, nh_ref, nc_ref, loss_ref,
    tok, tgt, mtok, mtgt, gate, up, down,
    fa, fb, act, part, recv, tok_t, act_t, dout, dgate, dup,
    gg, gu, gd, ug, uu, ud, msend, mown, mrecv,
    hid_pad, hid_all, rec_part, rec_recv, rec_half, rec_full, sq, stat, stat_recv, cell_pad,
    lossv, loss_recv, loss_chip, loss_all,
    in_sem, out_sem, hid_s, hid_r, rec_s, rec_r, loss_s, loss_r, sib_s, sib_r,
):
    me = lax.axis_index("task")
    core = lax.axis_index("shard")
    sib = 1 - core
    toks, width = tok.shape
    ff = gate.shape[1]
    h = hid_pad.shape[1]
    r = rw_ref.shape[0]
    tb = toks // 2
    fbk = 256
    half = rec_half.shape[1]

    barrier = pltpu.get_barrier_semaphore()

    def peer(off):
        return lax.rem(me + off, n)

    @pl.loop(1, n)
    def _(off):
        pl.semaphore_signal(barrier, inc=1, device_id=(peer(off), core), device_id_type=MESH)

    pl.semaphore_signal(barrier, inc=1, device_id=(me, sib), device_id_type=MESH)

    ins = [
        pltpu.make_async_copy(src.at[0], dst, in_sem.at[i])
        for i, (src, dst) in enumerate(
            ((tok_hbm, tok), (gate_hbm, gate), (up_hbm, up), (down_hbm, down), (tgt_hbm, tgt), (mtok_hbm, mtok), (mtgt_hbm, mtgt))
        )
    ]
    for c in ins:
        c.start()

    hid_pad[...] = jnp.zeros_like(hid_pad)
    for t in range(3):
        hid_pad[t:t + 1, :] = hid_ref[t]
    cell_pad[...] = jnp.zeros_like(cell_pad)
    for t in range(3):
        cell_pad[t:t + 1, :] = cell_ref[t]
    sq[...] = jnp.zeros_like(sq)
    hid_all[me] = hid_pad[...]

    def to_task(src, dst, ss, rs, who, slot):
        return pltpu.make_async_remote_copy(
            src_ref=src, dst_ref=dst.at[slot], send_sem=ss.at[who], recv_sem=rs.at[slot],
            device_id=(who, core), device_id_type=MESH,
        )

    def to_sib(src, dst, i):
        return pltpu.make_async_remote_copy(
            src_ref=src, dst_ref=dst, send_sem=sib_s.at[i], recv_sem=sib_r.at[i],
            device_id=(me, sib), device_id_type=MESH,
        )

    pl.semaphore_wait(barrier, n)

    @pl.loop(1, n)
    def _(off):
        to_task(hid_pad, hid_all, hid_s, hid_r, peer(off), me).start()

    ins[0].wait()
    ins[1].wait()
    ins[2].wait()

    def hidden(x, w1, w2, keep, beside=None):
        @pl.loop(0, ff // fbk)
        def _(j):
            fs = pl.ds(pl.multiple_of(j * fbk, fbk), fbk)
            for i in range(2):
                ts = pl.ds(i * tb, tb)
                g = dot(x[ts, :], w1[:, fs])
                u = dot(x[ts, :], w2[:, fs])
                s = jax.nn.sigmoid(g)
                a = g * s
                act[ts, fs] = (a * u).astype(bf16)
                if keep:
                    fa[ts, fs] = a
                    fb[ts, fs] = u * s * (1.0 + g * (1.0 - s))
                if beside is not None:
                    beside(2 * j + i, fbk // 2)

    hidden(tok, gate, up, True)
    ins[3].wait()
    for i in range(2):
        part[i] = dot(act[pl.ds(i * tb, tb), :], down[...])
        to_sib(part.at[i], recv.at[i], i).start()

    @pl.loop(1, n)
    def _(off):
        s = peer(off)
        to_task(hid_pad, hid_all, hid_s, hid_r, s, s).wait_recv()

    picks = lax.broadcasted_iota(jnp.int32, (h, r), 0) == lax.broadcasted_iota(jnp.int32, (h, r), 1) + me * r
    mine = dot(hid_all[...].reshape(n * 8, h), picks.astype(f32), precision=highest)
    cols = pl.ds(pl.multiple_of(core * half, half), half)
    rec_part[...] = dot(mine, rw_ref[:, cols], precision=highest).reshape(n, 8, half)

    @pl.loop(1, n)
    def _(off):
        s = peer(off)
        to_task(rec_part.at[s], rec_recv, rec_s, rec_r, s, me).start()

    rec_recv[me] = rec_part[me]

    tok_t[...] = tok[...].T
    act_t[...] = act[...].T

    def param_sq(w, slot):
        @pl.loop(0, w.shape[0] // 64)
        def _(k):
            x = w[pl.ds(pl.multiple_of(k * 64, 64), 64), :].astype(f32)
            x = fold_sq(x)
            sq[slot] += sum(x[:, q * fbk:(q + 1) * fbk] for q in range(x.shape[1] // fbk))

    param_sq(gate, 3)
    param_sq(up, 4)
    param_sq(down, 5)

    ins[4].wait()
    for i in range(2):
        to_sib(part.at[i], recv.at[i], i).wait()
        ts = pl.ds(i * tb, tb)

        @pl.loop(0, tb // 16)
        def _(k):
            rows = pl.ds(pl.multiple_of(k * 16, 16), 16)
            whole = pl.ds(pl.multiple_of(i * tb + k * 16, 16), 16)
            dout[whole, :] = (part[i, rows, :] + recv[i, rows, :] - tgt[whole, :].astype(f32)).astype(bf16)

        @pl.loop(0, ff // fbk)
        def _(j):
            fs = pl.ds(pl.multiple_of(j * fbk, fbk), fbk)
            d_act = dot(dout[ts, :], down[fs, :], ((1,), (1,)))
            dgate[ts, fs] = (d_act * fb[ts, fs]).astype(bf16)
            dup[ts, fs] = (d_act * fa[ts, fs]).astype(bf16)

    def grad(lhs, rhs, out, slot):
        @pl.loop(0, rhs.shape[1] // fbk)
        def _(j):
            fs = pl.ds(pl.multiple_of(j * fbk, fbk), fbk)
            for q in range(lhs.shape[0] // 256):
                rows = pl.ds(q * 256, 256)
                g = dot(lhs[rows, :], rhs[:, fs])
                out[rows, fs] = g
                sq[slot] += fold_sq(g)

    grad(tok_t, dgate, gg, 0)
    grad(tok_t, dup, gu, 1)
    grad(act_t, dout, gd, 2)

    stat[...] = jnp.zeros_like(stat)
    for i in range(6):
        stat[i // 3, i % 3:i % 3 + 1, :] = jnp.broadcast_to(total(sq[i]), (1, 128))
    to_sib(stat, stat_recv, 2).start()

    @pl.loop(1, n)
    def _(off):
        s = peer(off)
        to_task(rec_part.at[s], rec_recv, rec_s, rec_r, s, s).wait_recv()

    rec_half[...] = jnp.sum(rec_recv[...], axis=0)
    to_sib(rec_half, rec_full.at[core], 3).start()
    rec_full[core] = rec_half[...]

    to_sib(stat, stat_recv, 2).wait()
    entries = float(width * ff * lax.axis_size("shard"))
    rms = jnp.sqrt((stat[...] + stat_recv[...]) / entries + epsilon)
    rms_g, rms_p = rms[0], rms[1]
    lg, lp = jnp.log(rms_g)[:, 0:1], jnp.log(rms_p)[:, 0:1]
    frac = step_ref[0].astype(f32) / STEPS
    pltpu.make_async_remote_copy(
        src_ref=rec_half, dst_ref=rec_full.at[sib], send_sem=sib_s.at[3], recv_sem=sib_r.at[3],
        device_id=(me, sib), device_id_type=MESH,
    ).wait()

    def block(q):
        qs = pl.ds(q * h, h)
        rec = rec_full[(q * h) // half, :, pl.ds((q * h) % half, h)]
        return lg * iw_ref[0:1, qs] + lp * iw_ref[1:2, qs] + frac * iw_ref[2:3, qs] + rec + bias_ref[0:1, qs]

    cell = jax.nn.sigmoid(block(1)) * cell_pad[...] + jax.nn.sigmoid(block(0)) * jnp.tanh(block(2))
    hid = jax.nn.sigmoid(block(3)) * jnp.tanh(cell)
    for t in range(3):
        nc_ref[t] = cell[t:t + 1]
        nh_ref[t] = hid[t:t + 1]
    ctx = dot(hid, cw_ref[...], ((1,), (1,)), precision=highest)

    units = mlp_ref.shape[1]

    def coefs(t):
        rp, rg = rms_p[t:t + 1, 0:1], rms_g[t:t + 1, 0:1]
        ca = [mlp_ref[0, k] / rp for k in range(units)]
        cb = [mlp_ref[1, k] / rg for k in range(units)]
        cc = [ctx[t:t + 1, k:k + 1] for k in range(units)]
        return ca, cb, cc, jnp.exp(ctx[t:t + 1, units:units + 1]), rate_factor * rp

    def update(co, w, g, out, first, count):
        ca, cb, cc, size, back = co
        for i in range(count // 16):
            rows = pl.ds(pl.multiple_of(first + i * 16, 16), 16)
            for q in range(w.shape[1] // 256):
                qs = pl.ds(q * 256, 256)
                p = w[rows, qs].astype(f32)
                gv = g[rows, qs]
                acc = None
                for k in range(units):
                    term = mlp_ref[2, k] * jnp.maximum(ca[k] * p + cb[k] * gv + cc[k], 0.0)
                    acc = term if acc is None else acc + term
                upd = size * acc
                out[rows, qs] = upd.astype(bf16)
                w[rows, qs] = (p - back * upd).astype(bf16)

    outs = []
    for t, (w, g, o, oh) in enumerate(((gate, gg, ug, gu_hbm), (up, gu, uu, uu_hbm))):
        co = coefs(t)

        @pl.loop(0, w.shape[0] // 32)
        def _(i):
            update(co, w, g, o, i * 32, 32)

        c = pltpu.make_async_copy(o, oh.at[0], out_sem.at[t])
        c.start()
        outs.append(c)

    co = coefs(2)

    ins[5].wait()
    hidden(mtok, gate, up, False, lambda i, c: update(co, down, gd, ud, i * c, c))
    c = pltpu.make_async_copy(ud, du_hbm.at[0], out_sem.at[2])
    c.start()
    outs.append(c)
    msend[...] = dot(act[pl.ds(pl.multiple_of(sib * tb, tb), tb), :], down[...])
    to_sib(msend, mrecv, 4).start()
    own = pl.multiple_of(core * tb, tb)
    mown[...] = dot(act[pl.ds(own, tb), :], down[...])
    ins[6].wait()
    to_sib(msend, mrecv, 4).wait()
    lossv[...] = jnp.zeros_like(lossv)

    @pl.loop(0, tb // 16)
    def _(k):
        rows = pl.ds(pl.multiple_of(k * 16, 16), 16)
        d = mown[rows, :] + mrecv[rows, :] - mtgt[pl.ds(pl.multiple_of(own + k * 16, 16), 16), :].astype(f32)
        d = fold_sq(d)
        lossv[...] += sum(d[:, q * 128:(q + 1) * 128] for q in range(width // 128))

    to_sib(lossv, loss_recv, 5).start()
    to_sib(lossv, loss_recv, 5).wait()
    chip = lossv[...] + loss_recv[...]
    loss_chip[...] = chip
    loss_all[me] = chip

    @pl.loop(1, n)
    def _(off):
        to_task(loss_chip, loss_all, loss_s, loss_r, peer(off), me).start()

    for c in outs:
        c.wait()

    @pl.loop(1, n)
    def _(off):
        s = peer(off)
        to_task(hid_pad, hid_all, hid_s, hid_r, s, me).wait_send()
        to_task(rec_part.at[s], rec_recv, rec_s, rec_r, s, me).wait_send()
        to_task(loss_chip, loss_all, loss_s, loss_r, s, me).wait_send()
        to_task(loss_chip, loss_all, loss_s, loss_r, s, s).wait_recv()

    loss_ref[0, 0] = jnp.sum(jnp.sum(loss_all[...], axis=0)) * (0.5 / (toks * width)) / n


def local(*args):
    n = lax.axis_size("task")
    (tokens, targets, mtokens, mtargets, gate, up, down, step, hid, cell, rw, iw, bias, cw, mlp) = args
    toks, width = tokens.shape[1:]
    ff = gate.shape[2]
    h = hid.shape[2]
    r = rw.shape[0]
    half = rw.shape[1] // 2
    vm = pl.BlockSpec(memory_space=pltpu.VMEM)
    sm = pl.BlockSpec(memory_space=pltpu.SMEM)
    anys = pl.BlockSpec(memory_space=pl.ANY)
    V = pltpu.VMEM
    dma = pltpu.SemaphoreType.DMA
    tb = toks // 2
    outs = pl.pallas_call(
        functools.partial(kernel, n),
        out_shape=(
            jax.ShapeDtypeStruct(gate.shape, bf16),
            jax.ShapeDtypeStruct(up.shape, bf16),
            jax.ShapeDtypeStruct(down.shape, bf16),
            jax.ShapeDtypeStruct((hid.shape[1], 1, h), f32),
            jax.ShapeDtypeStruct((hid.shape[1], 1, h), f32),
            jax.ShapeDtypeStruct((1, 1), f32),
        ),
        in_specs=[pl.BlockSpec(memory_space=pltpu.HBM)] * 7 + [sm] + [vm] * 6 + [sm],
        out_specs=(anys, anys, anys, vm, vm, sm),
        scratch_shapes=[
            V((toks, width), bf16), V((toks, width), bf16), V((toks, width), bf16), V((toks, width), bf16),
            V((width, ff), bf16), V((width, ff), bf16), V((ff, width), bf16),
            V((toks, ff), f32), V((toks, ff), f32), V((toks, ff), bf16),
            V((2, tb, width), f32), V((2, tb, width), f32),
            V((width, toks), bf16), V((ff, toks), bf16), V((toks, width), bf16),
            V((toks, ff), bf16), V((toks, ff), bf16),
            V((width, ff), f32), V((width, ff), f32), V((ff, width), f32),
            V((width, ff), bf16), V((width, ff), bf16), V((ff, width), bf16),
            V((tb, width), f32), V((tb, width), f32), V((tb, width), f32),
            V((8, h), f32), V((n, 8, h), f32), V((n, 8, half), f32), V((n, 8, half), f32),
            V((8, half), f32), V((2, 8, half), f32),
            V((6, 8, 256), f32), V((2, 8, 128), f32), V((2, 8, 128), f32), V((8, h), f32),
            V((8, 128), f32), V((8, 128), f32), V((8, 128), f32), V((n, 8, 128), f32),
            dma((7,)), dma((3,)), dma((n,)), dma((n,)), dma((n,)), dma((n,)), dma((n,)), dma((n,)),
            dma((6,)), dma((6,)),
        ],
        compiler_params=pltpu.CompilerParams(
            collective_id=0, has_side_effects=True, vmem_limit_bytes=58 * 1024 * 1024
        ),
    )(tokens, targets, mtokens, mtargets, gate, up, down, step, jnp.swapaxes(hid, 0, 1), jnp.swapaxes(cell, 0, 1), rw, iw, bias[None], cw.T, mlp)
    return (*outs[:3], jnp.swapaxes(outs[3], 0, 1), jnp.swapaxes(outs[4], 0, 1), outs[5][0, 0])


def solution(mesh):
    return jax.shard_map(
        local,
        mesh=mesh,
        in_specs=(
            P("task", None, None),
            P("task", None, None),
            P("task", None, None),
            P("task", None, None),
            P("task", None, "shard"),
            P("task", None, "shard"),
            P("task", "shard", None),
            P("task"),
            P("task", None, None),
            P("task", None, None),
            P("task", None),
            P(),
            P(),
            P(),
            P(),
        ),
        out_specs=(
            P("task", None, "shard"),
            P("task", None, "shard"),
            P("task", "shard", None),
            P("task", None, None),
            P("task", None, None),
            P(),
        ),
        check_vma=False,
    )
```

```python
import functools

import jax
import jax.numpy as jnp
from jax import lax
from jax.experimental import pallas as pl
from jax.experimental.pallas import tpu as pltpu
from jax.sharding import PartitionSpec as P

STEPS = 10000

highest = lax.Precision.HIGHEST
epsilon = 1e-06
rate_factor = 0.1
f32 = jnp.float32
bf16 = jnp.bfloat16
MESH = pl.DeviceIdType.MESH


def dot(a, b, dims=((1,), (0,)), precision=None):
    return lax.dot_general(a, b, (dims, ((), ())), preferred_element_type=f32, precision=precision)


def fold_sq(x):
    x = x * x
    return jnp.sum(x.reshape(x.shape[0] // 8, 8, x.shape[1]), axis=0)


def total(x):
    return jnp.sum(jnp.sum(x, axis=1, keepdims=True), axis=0, keepdims=True)


def kernel(
    n,
    tok_hbm, tgt_hbm, mtok_hbm, mtgt_hbm, gate_hbm, up_hbm, down_hbm,
    step_ref, hid_ref, cell_ref, rw_ref, iw_ref, bias_ref, cw_ref, mlp_ref,
    gu_hbm, uu_hbm, du_hbm, nh_ref, nc_ref, loss_ref,
    tok, tgt, mtok, mtgt, gate, up, down,
    fa, fb, act, part, recv, tok_t, act_t, dout, dgate, dup,
    gg, gu, gd, ug, uu, ud, msend, mown, mrecv,
    hid_pad, hid_all, rec_part, rec_recv, rec_half, rec_full, sq, stat, stat_recv, cell_pad,
    lossv, loss_recv, loss_chip, loss_all,
    in_sem, out_sem, hid_s, hid_r, rec_s, rec_r, loss_s, loss_r, sib_s, sib_r,
):
    me = lax.axis_index("task")
    core = lax.axis_index("shard")
    sib = 1 - core
    toks, width = tok.shape
    ff = gate.shape[1]
    h = hid_pad.shape[1]
    r = rw_ref.shape[0]
    tb = toks // 2
    fbk = 256
    half = rec_half.shape[1]

    barrier = pltpu.get_barrier_semaphore()

    def peer(off):
        return lax.rem(me + off, n)

    @pl.loop(1, n)
    def _(off):
        pl.semaphore_signal(barrier, inc=1, device_id=(peer(off), core), device_id_type=MESH)

    pl.semaphore_signal(barrier, inc=1, device_id=(me, sib), device_id_type=MESH)

    ins = [
        pltpu.make_async_copy(src.at[0], dst, in_sem.at[i])
        for i, (src, dst) in enumerate(
            ((tok_hbm, tok), (gate_hbm, gate), (up_hbm, up), (down_hbm, down), (tgt_hbm, tgt), (mtok_hbm, mtok), (mtgt_hbm, mtgt))
        )
    ]
    for c in ins:
        c.start()

    hid_pad[...] = jnp.zeros_like(hid_pad)
    for t in range(3):
        hid_pad[t:t + 1, :] = hid_ref[t]
    cell_pad[...] = jnp.zeros_like(cell_pad)
    for t in range(3):
        cell_pad[t:t + 1, :] = cell_ref[t]
    sq[...] = jnp.zeros_like(sq)
    hid_all[me] = hid_pad[...]

    def to_task(src, dst, ss, rs, who, slot):
        return pltpu.make_async_remote_copy(
            src_ref=src, dst_ref=dst.at[slot], send_sem=ss.at[who], recv_sem=rs.at[slot],
            device_id=(who, core), device_id_type=MESH,
        )

    def to_sib(src, dst, i):
        return pltpu.make_async_remote_copy(
            src_ref=src, dst_ref=dst, send_sem=sib_s.at[i], recv_sem=sib_r.at[i],
            device_id=(me, sib), device_id_type=MESH,
        )

    pl.semaphore_wait(barrier, n)

    @pl.loop(1, n)
    def _(off):
        to_task(hid_pad, hid_all, hid_s, hid_r, peer(off), me).start()

    ins[0].wait()
    ins[1].wait()
    ins[2].wait()

    def hidden(x, w1, w2, keep, beside=None):
        @pl.loop(0, ff // fbk)
        def _(j):
            fs = pl.ds(pl.multiple_of(j * fbk, fbk), fbk)
            for i in range(2):
                ts = pl.ds(i * tb, tb)
                g = dot(x[ts, :], w1[:, fs])
                u = dot(x[ts, :], w2[:, fs])
                s = jax.nn.sigmoid(g)
                a = g * s
                act[ts, fs] = (a * u).astype(bf16)
                if keep:
                    fa[ts, fs] = a
                    fb[ts, fs] = u * s * (1.0 + g * (1.0 - s))
                if beside is not None:
                    beside(2 * j + i, fbk // 2)

    hidden(tok, gate, up, True)
    ins[3].wait()
    for i in range(2):
        part[i] = dot(act[pl.ds(i * tb, tb), :], down[...])
        to_sib(part.at[i], recv.at[i], i).start()

    @pl.loop(1, n)
    def _(off):
        s = peer(off)
        to_task(hid_pad, hid_all, hid_s, hid_r, s, s).wait_recv()

    picks = lax.broadcasted_iota(jnp.int32, (h, r), 0) == lax.broadcasted_iota(jnp.int32, (h, r), 1) + me * r
    mine = dot(hid_all[...].reshape(n * 8, h), picks.astype(f32), precision=highest)
    cols = pl.ds(pl.multiple_of(core * half, half), half)
    rec_part[...] = dot(mine, rw_ref[:, cols], precision=highest).reshape(n, 8, half)

    @pl.loop(1, n)
    def _(off):
        s = peer(off)
        to_task(rec_part.at[s], rec_recv, rec_s, rec_r, s, me).start()

    rec_recv[me] = rec_part[me]

    tok_t[...] = tok[...].T
    act_t[...] = act[...].T

    def param_sq(w, slot):
        @pl.loop(0, w.shape[0] // 64)
        def _(k):
            x = w[pl.ds(pl.multiple_of(k * 64, 64), 64), :].astype(f32)
            x = fold_sq(x)
            sq[slot] += sum(x[:, q * fbk:(q + 1) * fbk] for q in range(x.shape[1] // fbk))

    param_sq(gate, 3)
    param_sq(up, 4)
    param_sq(down, 5)

    ins[4].wait()
    for i in range(2):
        to_sib(part.at[i], recv.at[i], i).wait()
        ts = pl.ds(i * tb, tb)

        @pl.loop(0, tb // 16)
        def _(k):
            rows = pl.ds(pl.multiple_of(k * 16, 16), 16)
            whole = pl.ds(pl.multiple_of(i * tb + k * 16, 16), 16)
            dout[whole, :] = (part[i, rows, :] + recv[i, rows, :] - tgt[whole, :].astype(f32)).astype(bf16)

        @pl.loop(0, ff // fbk)
        def _(j):
            fs = pl.ds(pl.multiple_of(j * fbk, fbk), fbk)
            d_act = dot(dout[ts, :], down[fs, :], ((1,), (1,)))
            dgate[ts, fs] = (d_act * fb[ts, fs]).astype(bf16)
            dup[ts, fs] = (d_act * fa[ts, fs]).astype(bf16)

    def grad(lhs, rhs, out, slot):
        @pl.loop(0, rhs.shape[1] // fbk)
        def _(j):
            fs = pl.ds(pl.multiple_of(j * fbk, fbk), fbk)
            for q in range(lhs.shape[0] // 256):
                rows = pl.ds(q * 256, 256)
                g = dot(lhs[rows, :], rhs[:, fs])
                out[rows, fs] = g
                sq[slot] += fold_sq(g)

    grad(tok_t, dgate, gg, 0)
    grad(tok_t, dup, gu, 1)
    grad(act_t, dout, gd, 2)

    stat[...] = jnp.zeros_like(stat)
    for i in range(6):
        stat[i // 3, i % 3:i % 3 + 1, :] = jnp.broadcast_to(total(sq[i]), (1, 128))
    to_sib(stat, stat_recv, 2).start()

    @pl.loop(1, n)
    def _(off):
        s = peer(off)
        to_task(rec_part.at[s], rec_recv, rec_s, rec_r, s, s).wait_recv()

    rec_half[...] = jnp.sum(rec_recv[...], axis=0)
    to_sib(rec_half, rec_full.at[core], 3).start()
    rec_full[core] = rec_half[...]

    to_sib(stat, stat_recv, 2).wait()
    entries = float(width * ff * lax.axis_size("shard"))
    rms = jnp.sqrt((stat[...] + stat_recv[...]) / entries + epsilon)
    rms_g, rms_p = rms[0], rms[1]
    lg, lp = jnp.log(rms_g)[:, 0:1], jnp.log(rms_p)[:, 0:1]
    frac = step_ref[0].astype(f32) / STEPS
    pltpu.make_async_remote_copy(
        src_ref=rec_half, dst_ref=rec_full.at[sib], send_sem=sib_s.at[3], recv_sem=sib_r.at[3],
        device_id=(me, sib), device_id_type=MESH,
    ).wait()

    def block(q):
        qs = pl.ds(q * h, h)
        rec = rec_full[(q * h) // half, :, pl.ds((q * h) % half, h)]
        return lg * iw_ref[0:1, qs] + lp * iw_ref[1:2, qs] + frac * iw_ref[2:3, qs] + rec + bias_ref[0:1, qs]

    cell = jax.nn.sigmoid(block(1)) * cell_pad[...] + jax.nn.sigmoid(block(0)) * jnp.tanh(block(2))
    hid = jax.nn.sigmoid(block(3)) * jnp.tanh(cell)
    for t in range(3):
        nc_ref[t] = cell[t:t + 1]
        nh_ref[t] = hid[t:t + 1]
    ctx = dot(hid, cw_ref[...], ((1,), (1,)), precision=highest)

    units = mlp_ref.shape[1]

    def coefs(t):
        rp, rg = rms_p[t:t + 1, 0:1], rms_g[t:t + 1, 0:1]
        ca = [mlp_ref[0, k] / rp for k in range(units)]
        cb = [mlp_ref[1, k] / rg for k in range(units)]
        cc = [ctx[t:t + 1, k:k + 1] for k in range(units)]
        size = jnp.exp(ctx[t:t + 1, units:units + 1])
        one = lambda x: x[0, 0]
        return [one(x) for x in ca], [one(x) for x in cb], [one(x) for x in cc], one(size), one(rate_factor * rp)

    def update(co, w, g, out, first, count):
        ca, cb, cc, size, back = co
        for i in range(count // 16):
            rows = pl.ds(pl.multiple_of(first + i * 16, 16), 16)
            for q in range(w.shape[1] // 256):
                qs = pl.ds(q * 256, 256)
                p = w[rows, qs].astype(f32)
                gv = g[rows, qs]
                acc = None
                for k in range(units):
                    term = mlp_ref[2, k] * jnp.maximum(ca[k] * p + cb[k] * gv + cc[k], 0.0)
                    acc = term if acc is None else acc + term
                upd = size * acc
                out[rows, qs] = upd.astype(bf16)
                w[rows, qs] = (p - back * upd).astype(bf16)

    outs = []
    for t, (w, g, o, oh) in enumerate(((gate, gg, ug, gu_hbm), (up, gu, uu, uu_hbm))):
        co = coefs(t)

        @pl.loop(0, w.shape[0] // 64)
        def _(i):
            update(co, w, g, o, i * 64, 64)

        c = pltpu.make_async_copy(o, oh.at[0], out_sem.at[t])
        c.start()
        outs.append(c)

    co = coefs(2)

    ins[5].wait()
    hidden(mtok, gate, up, False, lambda i, c: update(co, down, gd, ud, i * c, c))
    c = pltpu.make_async_copy(ud, du_hbm.at[0], out_sem.at[2])
    c.start()
    outs.append(c)
    msend[...] = dot(act[pl.ds(pl.multiple_of(sib * tb, tb), tb), :], down[...])
    to_sib(msend, mrecv, 4).start()
    own = pl.multiple_of(core * tb, tb)
    mown[...] = dot(act[pl.ds(own, tb), :], down[...])
    ins[6].wait()
    to_sib(msend, mrecv, 4).wait()
    lossv[...] = jnp.zeros_like(lossv)

    @pl.loop(0, tb // 16)
    def _(k):
        rows = pl.ds(pl.multiple_of(k * 16, 16), 16)
        d = mown[rows, :] + mrecv[rows, :] - mtgt[pl.ds(pl.multiple_of(own + k * 16, 16), 16), :].astype(f32)
        d = fold_sq(d)
        lossv[...] += sum(d[:, q * 128:(q + 1) * 128] for q in range(width // 128))

    to_sib(lossv, loss_recv, 5).start()
    to_sib(lossv, loss_recv, 5).wait()
    chip = lossv[...] + loss_recv[...]
    loss_chip[...] = chip
    loss_all[me] = chip

    @pl.loop(1, n)
    def _(off):
        to_task(loss_chip, loss_all, loss_s, loss_r, peer(off), me).start()

    for c in outs:
        c.wait()

    @pl.loop(1, n)
    def _(off):
        s = peer(off)
        to_task(hid_pad, hid_all, hid_s, hid_r, s, me).wait_send()
        to_task(rec_part.at[s], rec_recv, rec_s, rec_r, s, me).wait_send()
        to_task(loss_chip, loss_all, loss_s, loss_r, s, me).wait_send()
        to_task(loss_chip, loss_all, loss_s, loss_r, s, s).wait_recv()

    loss_ref[0, 0] = jnp.sum(jnp.sum(loss_all[...], axis=0)) * (0.5 / (toks * width)) / n


def local(*args):
    n = lax.axis_size("task")
    (tokens, targets, mtokens, mtargets, gate, up, down, step, hid, cell, rw, iw, bias, cw, mlp) = args
    toks, width = tokens.shape[1:]
    ff = gate.shape[2]
    h = hid.shape[2]
    r = rw.shape[0]
    half = rw.shape[1] // 2
    vm = pl.BlockSpec(memory_space=pltpu.VMEM)
    sm = pl.BlockSpec(memory_space=pltpu.SMEM)
    anys = pl.BlockSpec(memory_space=pl.ANY)
    V = pltpu.VMEM
    dma = pltpu.SemaphoreType.DMA
    tb = toks // 2
    outs = pl.pallas_call(
        functools.partial(kernel, n),
        out_shape=(
            jax.ShapeDtypeStruct(gate.shape, bf16),
            jax.ShapeDtypeStruct(up.shape, bf16),
            jax.ShapeDtypeStruct(down.shape, bf16),
            jax.ShapeDtypeStruct((hid.shape[1], 1, h), f32),
            jax.ShapeDtypeStruct((hid.shape[1], 1, h), f32),
            jax.ShapeDtypeStruct((1, 1), f32),
        ),
        in_specs=[pl.BlockSpec(memory_space=pltpu.HBM)] * 7 + [sm] + [vm] * 6 + [sm],
        out_specs=(anys, anys, anys, vm, vm, sm),
        scratch_shapes=[
            V((toks, width), bf16), V((toks, width), bf16), V((toks, width), bf16), V((toks, width), bf16),
            V((width, ff), bf16), V((width, ff), bf16), V((ff, width), bf16),
            V((toks, ff), f32), V((toks, ff), f32), V((toks, ff), bf16),
            V((2, tb, width), f32), V((2, tb, width), f32),
            V((width, toks), bf16), V((ff, toks), bf16), V((toks, width), bf16),
            V((toks, ff), bf16), V((toks, ff), bf16),
            V((width, ff), f32), V((width, ff), f32), V((ff, width), f32),
            V((width, ff), bf16), V((width, ff), bf16), V((ff, width), bf16),
            V((tb, width), f32), V((tb, width), f32), V((tb, width), f32),
            V((8, h), f32), V((n, 8, h), f32), V((n, 8, half), f32), V((n, 8, half), f32),
            V((8, half), f32), V((2, 8, half), f32),
            V((6, 8, 256), f32), V((2, 8, 128), f32), V((2, 8, 128), f32), V((8, h), f32),
            V((8, 128), f32), V((8, 128), f32), V((8, 128), f32), V((n, 8, 128), f32),
            dma((7,)), dma((3,)), dma((n,)), dma((n,)), dma((n,)), dma((n,)), dma((n,)), dma((n,)),
            dma((6,)), dma((6,)),
        ],
        compiler_params=pltpu.CompilerParams(
            collective_id=0, has_side_effects=True, vmem_limit_bytes=58 * 1024 * 1024
        ),
    )(tokens, targets, mtokens, mtargets, gate, up, down, step, jnp.swapaxes(hid, 0, 1), jnp.swapaxes(cell, 0, 1), rw, iw, bias[None], cw.T, mlp)
    return (*outs[:3], jnp.swapaxes(outs[3], 0, 1), jnp.swapaxes(outs[4], 0, 1), outs[5][0, 0])


def solution(mesh):
    return jax.shard_map(
        local,
        mesh=mesh,
        in_specs=(
            P("task", None, None),
            P("task", None, None),
            P("task", None, None),
            P("task", None, None),
            P("task", None, "shard"),
            P("task", None, "shard"),
            P("task", "shard", None),
            P("task"),
            P("task", None, None),
            P("task", None, None),
            P("task", None),
            P(),
            P(),
            P(),
            P(),
        ),
        out_specs=(
            P("task", None, "shard"),
            P("task", None, "shard"),
            P("task", "shard", None),
            P("task", None, None),
            P("task", None, None),
            P(),
        ),
        check_vma=False,
    )
```

```python
import functools

import jax
import jax.numpy as jnp
from jax import lax
from jax.experimental import pallas as pl
from jax.experimental.pallas import tpu as pltpu
from jax.sharding import PartitionSpec as P

STEPS = 10000

highest = lax.Precision.HIGHEST
epsilon = 1e-06
rate_factor = 0.1
f32 = jnp.float32
bf16 = jnp.bfloat16
MESH = pl.DeviceIdType.MESH


def dot(a, b, dims=((1,), (0,)), precision=None):
    return lax.dot_general(a, b, (dims, ((), ())), preferred_element_type=f32, precision=precision)


def fold_sq(x):
    x = x * x
    return jnp.sum(x.reshape(x.shape[0] // 8, 8, x.shape[1]), axis=0)


def total(x):
    return jnp.sum(jnp.sum(x, axis=1, keepdims=True), axis=0, keepdims=True)


def kernel(
    n,
    tok_hbm, tgt_hbm, mtok_hbm, mtgt_hbm, gate_hbm, up_hbm, down_hbm,
    step_ref, hid_ref, cell_ref, rw_ref, iw_ref, bias_ref, cw_ref, mlp_ref,
    gu_hbm, uu_hbm, du_hbm, nh_ref, nc_ref, loss_ref,
    tok, tgt, mtok, mtgt, gate, up, down,
    fa, fb, act, part, recv, tok_t, act_t, dout, dgate, dup,
    gg, gu, gd, ug, uu, ud, msend, mown, mrecv,
    hid_pad, hid_all, rec_part, rec_recv, rec_half, rec_full, sq, stat, stat_recv, cell_pad,
    lossv, loss_recv, loss_chip, loss_all,
    in_sem, out_sem, hid_s, hid_r, rec_s, rec_r, loss_s, loss_r, sib_s, sib_r,
):
    me = lax.axis_index("task")
    core = lax.axis_index("shard")
    sib = 1 - core
    toks, width = tok.shape
    ff = gate.shape[1]
    h = hid_pad.shape[1]
    r = rw_ref.shape[0]
    tb = toks // 2
    fbk = 256
    half = rec_half.shape[1]

    barrier = pltpu.get_barrier_semaphore()

    def peer(off):
        return lax.rem(me + off, n)

    @pl.loop(1, n)
    def _(off):
        pl.semaphore_signal(barrier, inc=1, device_id=(peer(off), core), device_id_type=MESH)

    pl.semaphore_signal(barrier, inc=1, device_id=(me, sib), device_id_type=MESH)

    ins = [
        pltpu.make_async_copy(src.at[0], dst, in_sem.at[i])
        for i, (src, dst) in enumerate(
            ((tok_hbm, tok), (gate_hbm, gate), (up_hbm, up), (down_hbm, down), (tgt_hbm, tgt), (mtok_hbm, mtok), (mtgt_hbm, mtgt))
        )
    ]
    for c in ins:
        c.start()

    hid_pad[...] = jnp.zeros_like(hid_pad)
    for t in range(3):
        hid_pad[t:t + 1, :] = hid_ref[t]
    cell_pad[...] = jnp.zeros_like(cell_pad)
    for t in range(3):
        cell_pad[t:t + 1, :] = cell_ref[t]
    sq[...] = jnp.zeros_like(sq)
    hid_all[me] = hid_pad[...]

    def to_task(src, dst, ss, rs, who, slot):
        return pltpu.make_async_remote_copy(
            src_ref=src, dst_ref=dst.at[slot], send_sem=ss.at[who], recv_sem=rs.at[slot],
            device_id=(who, core), device_id_type=MESH,
        )

    def to_sib(src, dst, i):
        return pltpu.make_async_remote_copy(
            src_ref=src, dst_ref=dst, send_sem=sib_s.at[i], recv_sem=sib_r.at[i],
            device_id=(me, sib), device_id_type=MESH,
        )

    pl.semaphore_wait(barrier, n)

    @pl.loop(1, n)
    def _(off):
        to_task(hid_pad, hid_all, hid_s, hid_r, peer(off), me).start()

    ins[0].wait()
    ins[1].wait()
    ins[2].wait()

    def hidden(x, w1, w2, keep, beside=None):
        @pl.loop(0, ff // fbk)
        def _(j):
            fs = pl.ds(pl.multiple_of(j * fbk, fbk), fbk)
            for i in range(2):
                ts = pl.ds(i * tb, tb)
                g = dot(x[ts, :], w1[:, fs])
                u = dot(x[ts, :], w2[:, fs])
                s = jax.nn.sigmoid(g)
                a = g * s
                act[ts, fs] = (a * u).astype(bf16)
                if keep:
                    fa[ts, fs] = a
                    fb[ts, fs] = u * s * (1.0 + g * (1.0 - s))
                if beside is not None:
                    beside(2 * j + i, fbk // 2)

    hidden(tok, gate, up, True)
    ins[3].wait()
    for i in range(2):
        part[i] = dot(act[pl.ds(i * tb, tb), :], down[...])
        to_sib(part.at[i], recv.at[i], i).start()

    @pl.loop(1, n)
    def _(off):
        s = peer(off)
        to_task(hid_pad, hid_all, hid_s, hid_r, s, s).wait_recv()

    picks = lax.broadcasted_iota(jnp.int32, (h, r), 0) == lax.broadcasted_iota(jnp.int32, (h, r), 1) + me * r
    mine = dot(hid_all[...].reshape(n * 8, h), picks.astype(f32), precision=highest)
    cols = pl.ds(pl.multiple_of(core * half, half), half)
    rec_part[...] = dot(mine, rw_ref[:, cols], precision=highest).reshape(n, 8, half)

    @pl.loop(1, n)
    def _(off):
        s = peer(off)
        to_task(rec_part.at[s], rec_recv, rec_s, rec_r, s, me).start()

    rec_recv[me] = rec_part[me]

    tok_t[...] = tok[...].T
    act_t[...] = act[...].T

    def param_sq(w, slot):
        @pl.loop(0, w.shape[0] // 64)
        def _(k):
            x = w[pl.ds(pl.multiple_of(k * 64, 64), 64), :].astype(f32)
            x = fold_sq(x)
            sq[slot] += sum(x[:, q * fbk:(q + 1) * fbk] for q in range(x.shape[1] // fbk))

    param_sq(gate, 3)
    param_sq(up, 4)
    param_sq(down, 5)

    ins[4].wait()
    for i in range(2):
        to_sib(part.at[i], recv.at[i], i).wait()
        ts = pl.ds(i * tb, tb)

        @pl.loop(0, tb // 16)
        def _(k):
            rows = pl.ds(pl.multiple_of(k * 16, 16), 16)
            whole = pl.ds(pl.multiple_of(i * tb + k * 16, 16), 16)
            dout[whole, :] = (part[i, rows, :] + recv[i, rows, :] - tgt[whole, :].astype(f32)).astype(bf16)

        @pl.loop(0, ff // fbk)
        def _(j):
            fs = pl.ds(pl.multiple_of(j * fbk, fbk), fbk)
            d_act = dot(dout[ts, :], down[fs, :], ((1,), (1,)))
            dgate[ts, fs] = (d_act * fb[ts, fs]).astype(bf16)
            dup[ts, fs] = (d_act * fa[ts, fs]).astype(bf16)

    def grad(lhs, rhs, out, slot):
        @pl.loop(0, rhs.shape[1] // fbk)
        def _(j):
            fs = pl.ds(pl.multiple_of(j * fbk, fbk), fbk)
            for q in range(lhs.shape[0] // 256):
                rows = pl.ds(q * 256, 256)
                g = dot(lhs[rows, :], rhs[:, fs])
                out[rows, fs] = g
                sq[slot] += fold_sq(g)

    grad(tok_t, dgate, gg, 0)
    grad(tok_t, dup, gu, 1)
    grad(act_t, dout, gd, 2)

    stat[...] = jnp.zeros_like(stat)
    for i in range(6):
        stat[i // 3, i % 3:i % 3 + 1, :] = jnp.broadcast_to(total(sq[i]), (1, 128))
    to_sib(stat, stat_recv, 2).start()

    @pl.loop(1, n)
    def _(off):
        s = peer(off)
        to_task(rec_part.at[s], rec_recv, rec_s, rec_r, s, s).wait_recv()

    rec_half[...] = jnp.sum(rec_recv[...], axis=0)
    to_sib(rec_half, rec_full.at[core], 3).start()
    rec_full[core] = rec_half[...]

    to_sib(stat, stat_recv, 2).wait()
    entries = float(width * ff * lax.axis_size("shard"))
    rms = jnp.sqrt((stat[...] + stat_recv[...]) / entries + epsilon)
    rms_g, rms_p = rms[0], rms[1]
    lg, lp = jnp.log(rms_g)[:, 0:1], jnp.log(rms_p)[:, 0:1]
    frac = step_ref[0].astype(f32) / STEPS
    pltpu.make_async_remote_copy(
        src_ref=rec_half, dst_ref=rec_full.at[sib], send_sem=sib_s.at[3], recv_sem=sib_r.at[3],
        device_id=(me, sib), device_id_type=MESH,
    ).wait()

    def block(q):
        qs = pl.ds(q * h, h)
        rec = rec_full[(q * h) // half, :, pl.ds((q * h) % half, h)]
        return lg * iw_ref[0:1, qs] + lp * iw_ref[1:2, qs] + frac * iw_ref[2:3, qs] + rec + bias_ref[0:1, qs]

    cell = jax.nn.sigmoid(block(1)) * cell_pad[...] + jax.nn.sigmoid(block(0)) * jnp.tanh(block(2))
    hid = jax.nn.sigmoid(block(3)) * jnp.tanh(cell)
    for t in range(3):
        nc_ref[t] = cell[t:t + 1]
        nh_ref[t] = hid[t:t + 1]
    ctx = dot(hid, cw_ref[...], ((1,), (1,)), precision=highest)

    units = mlp_ref.shape[1]

    def coefs(t):
        rp, rg = rms_p[t:t + 1, 0:1], rms_g[t:t + 1, 0:1]
        ca = [mlp_ref[0, k] / rp for k in range(units)]
        cb = [mlp_ref[1, k] / rg for k in range(units)]
        cc = [ctx[t:t + 1, k:k + 1] for k in range(units)]
        size = jnp.exp(ctx[t:t + 1, units:units + 1])
        one = lambda x: x[0, 0]
        return [one(x) for x in ca], [one(x) for x in cb], [one(x) for x in cc], one(size), one(rate_factor * rp)

    def update(co, w, g, out, first, count):
        ca, cb, cc, size, back = co
        for i in range(count // 16):
            rows = pl.ds(pl.multiple_of(first + i * 16, 16), 16)
            for q in range(w.shape[1] // 256):
                qs = pl.ds(q * 256, 256)
                p = w[rows, qs].astype(f32)
                gv = g[rows, qs]
                acc = None
                for k in range(units):
                    term = mlp_ref[2, k] * jnp.maximum(ca[k] * p + cb[k] * gv + cc[k], 0.0)
                    acc = term if acc is None else acc + term
                upd = size * acc
                out[rows, qs] = upd.astype(bf16)
                w[rows, qs] = (p - back * upd).astype(bf16)

    outs = []
    for t, (w, g, o, oh) in enumerate(((gate, gg, ug, gu_hbm), (up, gu, uu, uu_hbm))):
        co = coefs(t)

        @pl.loop(0, w.shape[0] // 64)
        def _(i):
            update(co, w, g, o, i * 64, 64)

        c = pltpu.make_async_copy(o, oh.at[0], out_sem.at[t])
        c.start()
        outs.append(c)

    co = coefs(2)

    ins[5].wait()
    hidden(mtok, gate, up, False, lambda i, c: update(co, down, gd, ud, i * c, c))
    c = pltpu.make_async_copy(ud, du_hbm.at[0], out_sem.at[2])
    c.start()
    outs.append(c)
    msend[...] = dot(act[pl.ds(pl.multiple_of(sib * tb, tb), tb), :], down[...])
    to_sib(msend, mrecv, 4).start()
    own = pl.multiple_of(core * tb, tb)
    mown[...] = dot(act[pl.ds(own, tb), :], down[...])
    ins[6].wait()
    to_sib(msend, mrecv, 4).wait()
    lossv[...] = jnp.zeros_like(lossv)

    @pl.loop(0, tb // 16)
    def _(k):
        rows = pl.ds(pl.multiple_of(k * 16, 16), 16)
        d = mown[rows, :] + mrecv[rows, :] - mtgt[pl.ds(pl.multiple_of(own + k * 16, 16), 16), :].astype(f32)
        d = fold_sq(d)
        lossv[...] += sum(d[:, q * 128:(q + 1) * 128] for q in range(width // 128))

    to_sib(lossv, loss_recv, 5).start()
    to_sib(lossv, loss_recv, 5).wait()
    chip = lossv[...] + loss_recv[...]
    loss_chip[...] = chip
    loss_all[me] = chip

    @pl.loop(1, n)
    def _(off):
        to_task(loss_chip, loss_all, loss_s, loss_r, peer(off), me).start()

    for c in outs:
        c.wait()

    @pl.loop(1, n)
    def _(off):
        s = peer(off)
        to_task(hid_pad, hid_all, hid_s, hid_r, s, me).wait_send()
        to_task(rec_part.at[s], rec_recv, rec_s, rec_r, s, me).wait_send()
        to_task(loss_chip, loss_all, loss_s, loss_r, s, me).wait_send()
        to_task(loss_chip, loss_all, loss_s, loss_r, s, s).wait_recv()

    loss_ref[0, 0] = jnp.sum(jnp.sum(loss_all[...], axis=0)) * (0.5 / (toks * width)) / n


def hand_out(count, *refs):
    srcs, dsts, bufs = refs[:count], refs[count:2 * count], refs[2 * count:3 * count]
    in_sem, out_sem = refs[3 * count:]
    loads, stores = [], []
    for i in range(count):
        rows = bufs[i].shape[0]
        parts = 2 if rows % 32 == 0 else 1
        for q in range(parts):
            rs = pl.ds(q * (rows // parts), rows // parts)
            loads.append(pltpu.make_async_copy(srcs[i].at[rs], bufs[i].at[rs], in_sem.at[2 * i + q]))
            stores.append(pltpu.make_async_copy(bufs[i].at[rs], dsts[i].at[rs], out_sem.at[2 * i + q]))
    for c in loads:
        c.start()
    for c, d in zip(loads, stores):
        c.wait()
        d.start()
    for d in stores:
        d.wait()


def local(*args):
    n = lax.axis_size("task")
    (tokens, targets, mtokens, mtargets, gate, up, down, step, hid, cell, rw, iw, bias, cw, mlp) = args
    toks, width = tokens.shape[1:]
    ff = gate.shape[2]
    h = hid.shape[2]
    r = rw.shape[0]
    half = rw.shape[1] // 2
    vm = pl.BlockSpec(memory_space=pltpu.VMEM)
    sm = pl.BlockSpec(memory_space=pltpu.SMEM)
    anys = pl.BlockSpec(memory_space=pl.ANY)
    V = pltpu.VMEM
    dma = pltpu.SemaphoreType.DMA
    tb = toks // 2
    outs = pl.pallas_call(
        functools.partial(kernel, n),
        out_shape=(
            jax.ShapeDtypeStruct(gate.shape, bf16),
            jax.ShapeDtypeStruct(up.shape, bf16),
            jax.ShapeDtypeStruct(down.shape, bf16),
            jax.ShapeDtypeStruct((hid.shape[1], 1, h), f32),
            jax.ShapeDtypeStruct((hid.shape[1], 1, h), f32),
            jax.ShapeDtypeStruct((1, 1), f32),
        ),
        in_specs=[pl.BlockSpec(memory_space=pltpu.HBM)] * 7 + [sm] + [vm] * 6 + [sm],
        out_specs=(anys, anys, anys, vm, vm, sm),
        scratch_shapes=[
            V((toks, width), bf16), V((toks, width), bf16), V((toks, width), bf16), V((toks, width), bf16),
            V((width, ff), bf16), V((width, ff), bf16), V((ff, width), bf16),
            V((toks, ff), f32), V((toks, ff), f32), V((toks, ff), bf16),
            V((2, tb, width), f32), V((2, tb, width), f32),
            V((width, toks), bf16), V((ff, toks), bf16), V((toks, width), bf16),
            V((toks, ff), bf16), V((toks, ff), bf16),
            V((width, ff), f32), V((width, ff), f32), V((ff, width), f32),
            V((width, ff), bf16), V((width, ff), bf16), V((ff, width), bf16),
            V((tb, width), f32), V((tb, width), f32), V((tb, width), f32),
            V((8, h), f32), V((n, 8, h), f32), V((n, 8, half), f32), V((n, 8, half), f32),
            V((8, half), f32), V((2, 8, half), f32),
            V((6, 8, 256), f32), V((2, 8, 128), f32), V((2, 8, 128), f32), V((8, h), f32),
            V((8, 128), f32), V((8, 128), f32), V((8, 128), f32), V((n, 8, 128), f32),
            dma((7,)), dma((3,)), dma((n,)), dma((n,)), dma((n,)), dma((n,)), dma((n,)), dma((n,)),
            dma((6,)), dma((6,)),
        ],
        compiler_params=pltpu.CompilerParams(
            collective_id=0, has_side_effects=True, vmem_limit_bytes=58 * 1024 * 1024
        ),
    )(tokens, targets, mtokens, mtargets, gate, up, down, step, jnp.swapaxes(hid, 0, 1), jnp.swapaxes(cell, 0, 1), rw, iw, bias[None], cw.T, mlp)
    sent = [x[0] for x in outs[:3]] + list(outs[3:5])
    moved = pl.pallas_call(
        functools.partial(hand_out, len(sent)),
        out_shape=tuple(jax.ShapeDtypeStruct(x.shape, x.dtype) for x in sent),
        in_specs=[anys] * len(sent),
        out_specs=(anys,) * len(sent),
        scratch_shapes=[V(x.shape, x.dtype) for x in sent] + [dma((2 * len(sent),)), dma((2 * len(sent),))],
        compiler_params=pltpu.CompilerParams(vmem_limit_bytes=58 * 1024 * 1024),
    )(*sent)
    outs = [x[None] for x in moved[:3]] + list(moved[3:]) + [outs[5]]
    return (*outs[:3], jnp.swapaxes(outs[3], 0, 1), jnp.swapaxes(outs[4], 0, 1), outs[5][0, 0])


def solution(mesh):
    return jax.shard_map(
        local,
        mesh=mesh,
        in_specs=(
            P("task", None, None),
            P("task", None, None),
            P("task", None, None),
            P("task", None, None),
            P("task", None, "shard"),
            P("task", None, "shard"),
            P("task", "shard", None),
            P("task"),
            P("task", None, None),
            P("task", None, None),
            P("task", None),
            P(),
            P(),
            P(),
            P(),
        ),
        out_specs=(
            P("task", None, "shard"),
            P("task", None, "shard"),
            P("task", "shard", None),
            P("task", None, None),
            P("task", None, None),
            P(),
        ),
        check_vma=False,
    )
```
